128 devices in a mesh: section: 4 (over z), dp: 32 (over y, x, core).
Axes of the slice: x: 4, y: 4, z: 4, core: 2. Of those that a mesh axis runs over, the one named last changes fastest.
Arguments:
- x_in: bfloat16 [32, 4, 128, 768], P('dp'), may hold values from -12 to 12
- cotangent: bfloat16 [32, 4, 128, 768], P('dp'), may hold values from -0.25 to 0.25
- w_in: bfloat16 [4, 768, 3072], P('section'), may hold values from -0.21875 to 0.21875
- w_out: bfloat16 [4, 768, 3072], P('section'), may hold values from -0.109375 to 0.109375
- gain: bfloat16 [4, 768], P('section'), may hold values from 0.099609375 to 1.8984375
- drop_mask: int32 [32, 4, 1, 4], P('dp'), may hold values 0 or 1
Outputs:
- grad_in: float32 [4, 768, 3072], P('section', 'dp')
- grad_out: float32 [4, 768, 3072], P('section', 'dp')
- grad_gain: float32 [4, 768], P('section', 'dp')
The draws below stay inside these ranges and needn't reach their ends.
All inputs are finite; a program needn't handle non-finite values. No bound on the sum of `drop_mask` on one device may be relied on, other than what follows from the above.
Results may differ from the reference program's by a relative error of at most 0.035.
Values may be sent and summed in bfloat16 or wider, within the bound.
No kernel may reach another device: no remote copies, remote signals or barrier semaphores. Data moves between devices by JAX's collectives and lax.ppermute only.
A program may use at most 256 MiB of HBM per device.

```python
import jax
import jax.numpy as jnp
from jax import lax

D = 768
HID = 3072
SEQ = 128
MICRO = 4
MB_SEQS = 1
ROWS = 128
LAYERS = 4
REPLICAS = 32


def set_ends(values, stream_key, smallest, largest):
    shape = values.shape
    place = [jax.random.randint(jax.random.fold_in(stream_key, axis), (), 0, shape[axis]) for axis in range(len(shape))]
    values = values.at[tuple(place)].set(smallest)
    longest = shape.index(max(shape))
    place[longest] = (place[longest] + 1) % shape[longest]
    return values.at[tuple(place)].set(largest)


def raised(values, stream_key, source, target, blocks, factor):
    def block_of(dim):
        return (jnp.arange(values.shape[dim]) // (values.shape[dim] // blocks)).reshape((-1,) + (1,) * (values.ndim - 1 - dim))

    first = jax.random.permutation(stream_key, blocks)[block_of(target)]
    other_side = (block_of(target) + blocks // 2) % blocks
    return jnp.where((block_of(source) == first) | (block_of(source) == other_side), factor * values, values)


def shard_levels(own_key, extent, cuts, least, high):
    level = 1.0
    for axis_at, shards_of in cuts:
        steps = jax.random.uniform(jax.random.fold_in(jax.random.fold_in(own_key, 6), axis_at), (shards_of,), jnp.float32, least / len(cuts), high / len(cuts))
        level = level * jnp.repeat(jnp.exp(steps), extent[axis_at] // shards_of).reshape((-1,) + (1,) * (len(extent) - 1 - axis_at))
    return level


def scatter_about(key, dims, scale, bound, cuts=(), dtype=jnp.bfloat16):
    array = scale * jax.random.normal(key, dims, jnp.float32)
    if cuts:
        array = array * shard_levels(key, dims, cuts, -0.22, 0.18)
    return jnp.clip(array, -bound, bound).astype(dtype)


def bell_draw_with(key, shape, spread, limit, shards, heavy, kind=jnp.bfloat16):
    result = spread * jax.random.normal(key, shape, jnp.float32)
    if shards:
        result = result * shard_levels(key, shape, shards, -0.22, 0.18)
    return jnp.clip(raised(result, jax.random.fold_in(key, 3), *heavy), -limit, limit).astype(kind)


def setup_inputs(seed: int = 0) -> dict:
    splits = jax.random.split(jax.random.key(seed), 7)
    x_in = bell_draw_with(splits[0], (REPLICAS, MICRO, ROWS, D), 1.0, 12.0, ((0, 32),), (0, 3, 32, 2.75))
    cotangent = bell_draw_with(splits[1], (REPLICAS, MICRO, ROWS, D), 0.02, 0.25, ((0, 32),), (0, 3, 32, 2.75))
    w_in = scatter_about(splits[2], (LAYERS, D, HID), D ** -0.5, 0.21875, ((0, 4),))
    w_out = scatter_about(splits[3], (LAYERS, D, HID), HID ** -0.5, 0.109375, ((0, 4),))
    gain = jnp.clip(1.0 + 0.18 * jax.random.normal(splits[4], (LAYERS, D), jnp.float32), 0.099609375, 1.8984375).astype(jnp.bfloat16)
    drop_mask = set_ends((jax.random.randint(splits[5], (REPLICAS, MICRO, MB_SEQS, LAYERS), 0, 4) < 3).astype(jnp.int32), jax.random.fold_in(splits[5], 1), 0, 1)
    return dict(x_in=x_in, cotangent=cotangent, w_in=w_in, w_out=w_out, gain=gain, drop_mask=drop_mask)


EPSILON = 1e-05
ROOT_HALF = 0.7071067811865476
DENSITY_SCALE = 0.3989422804014327

def gelu_exact(hidden):
    return 0.5 * hidden * (1.0 + lax.erf(hidden * ROOT_HALF))

def gelu_slope(hidden):
    return 0.5 * (1.0 + lax.erf(hidden * ROOT_HALF)) + hidden * jnp.exp(-0.5 * hidden * hidden) * DENSITY_SCALE

def block_forward(inputs, keep_rows, gain_row, w_first, w_second):
    as_float = inputs.astype(jnp.float32)
    inv_rms = lax.rsqrt(lax.optimization_barrier(jnp.mean(as_float * as_float, axis=-1, keepdims=True)) + EPSILON)
    normed = (as_float * inv_rms * gain_row.astype(jnp.float32)).astype(jnp.bfloat16)
    hidden = jnp.dot(normed, w_first, preferred_element_type=jnp.float32)
    active = gelu_exact(hidden).astype(jnp.bfloat16)
    branch = lax.dot_general(active, w_second, (((1,), (1,)), ((), ())), preferred_element_type=jnp.float32)
    outputs = (as_float + keep_rows[:, None] * branch).astype(jnp.bfloat16)
    return (outputs, normed, hidden, active, inv_rms)

def block_backward(upstream, inputs, keep_rows, gain_row, w_first, w_second, normed, hidden, active, inv_rms):
    up_float = upstream.astype(jnp.float32)
    gated = (keep_rows[:, None] * up_float).astype(jnp.bfloat16)
    grad_second = lax.dot_general(gated, active, (((0,), (0,)), ((), ())), preferred_element_type=jnp.float32)
    grad_active = jnp.dot(gated, w_second, preferred_element_type=jnp.float32)
    grad_hidden = (grad_active * gelu_slope(hidden)).astype(jnp.bfloat16)
    grad_first = lax.dot_general(normed, grad_hidden, (((0,), (0,)), ((), ())), preferred_element_type=jnp.float32)
    grad_normed = lax.dot_general(grad_hidden, w_first, (((1,), (1,)), ((), ())), preferred_element_type=jnp.float32)
    as_float = inputs.astype(jnp.float32)
    grad_gain = lax.optimization_barrier(jnp.sum(grad_normed * as_float * inv_rms, axis=0))
    scaled_grad = grad_normed * gain_row.astype(jnp.float32)
    centre = lax.optimization_barrier(jnp.mean(scaled_grad * as_float, axis=-1, keepdims=True))
    grad_inputs = up_float + inv_rms * (scaled_grad - as_float * inv_rms * inv_rms * centre)
    return (grad_inputs.astype(jnp.bfloat16), grad_first, grad_second, grad_gain)

def one_half(rows_in, rows_cot, keep_rows, w_in, w_out, gain):
    layers = w_in.shape[0]
    carried = rows_in
    saved_parts = []
    for layer_index in range(layers):
        outputs, normed, hidden, active, inv_rms = block_forward(carried, keep_rows[:, layer_index], gain[layer_index], w_in[layer_index], w_out[layer_index])
        saved_parts.append((carried, normed, hidden, active, inv_rms))
        carried = lax.optimization_barrier(outputs)
    upstream = rows_cot
    firsts = [None] * layers
    seconds = [None] * layers
    gains = [None] * layers
    for layer_index in range(layers - 1, -1, -1):
        inputs, normed, hidden, active, inv_rms = saved_parts[layer_index]
        grad_inputs, grad_first, grad_second, grad_gain = block_backward(upstream, inputs, keep_rows[:, layer_index], gain[layer_index], w_in[layer_index], w_out[layer_index], normed, hidden, active, inv_rms)
        firsts[layer_index] = grad_first
        seconds[layer_index] = grad_second
        gains[layer_index] = grad_gain
        upstream = lax.optimization_barrier(grad_inputs)
    return (jnp.stack(firsts), jnp.stack(seconds), jnp.stack(gains))

def rounded(value_sum):
    return lax.optimization_barrier(value_sum.astype(jnp.bfloat16)).astype(jnp.float32)

def reference(x_in, cotangent, w_in, w_out, gain, drop_mask):
    half_count = MICRO // 2
    model_width = w_in.shape[1]

    def replica(totals, replica_items):
        inputs, cot_rows, drop_marks = replica_items
        keep_table = jnp.repeat(drop_marks.astype(jnp.float32), SEQ, axis=1)
        halves = []
        for portion in range(2):
            start = portion * half_count
            rows_in = inputs[start:start + half_count].reshape(-1, model_width)
            rows_cot = cot_rows[start:start + half_count].reshape(-1, model_width)
            keep_rows = keep_table[start:start + half_count].reshape(rows_in.shape[0], -1)
            halves.append(one_half(rows_in, rows_cot, keep_rows, w_in, w_out, gain))
        parts = tuple((rounded(rounded(first) + rounded(second)) for first, second in zip(halves[0], halves[1])))
        totals = tuple((total + part for total, part in zip(totals, parts)))
        return (totals, None)
    zero_sums = (jnp.zeros(w_in.shape, jnp.float32), jnp.zeros(w_out.shape, jnp.float32), jnp.zeros(gain.shape, jnp.float32))
    totals, unused = lax.scan(replica, zero_sums, (x_in, cotangent, drop_mask))
    return (totals[0], totals[1], totals[2])
```

```python
import jax
import jax.numpy as jnp
import numpy as np
from jax import lax
from jax.experimental import pallas as pl
from jax.experimental.pallas import tpu as pltpu
from jax.sharding import PartitionSpec as P


EPSILON = 1e-05
ROOT_HALF = 0.7071067811865476
DENSITY_SCALE = 0.3989422804014327
BF = jnp.bfloat16
F32 = jnp.float32
STAGES = 4
LAG = 2
CHUNKS = 8
TILE = 512
PAD = 128
SIDE_X = 4
SIDE_Y = 4
MIB = 1024 * 1024

VMEM_SPEC = pl.BlockSpec(memory_space=pltpu.VMEM)
SMEM_SPEC = pl.BlockSpec(memory_space=pltpu.SMEM)


def vmem_call(kernel, outs, args, specs=None, aliases=None, limit=16, flops=0, moved=0, scratch=()):
    return pl.pallas_call(
        kernel,
        out_shape=tuple(pltpu.VMEM(shape, dtype) for shape, dtype in outs),
        in_specs=specs or [VMEM_SPEC] * len(args),
        out_specs=tuple(VMEM_SPEC for _ in outs),
        input_output_aliases=aliases or {},
        scratch_shapes=list(scratch),
        compiler_params=pltpu.CompilerParams(vmem_limit_bytes=limit * MIB),
        cost_estimate=pl.CostEstimate(flops=flops, bytes_accessed=moved, transcendentals=0),
    )(*args)


def nt_dot(a, b):
    return lax.dot_general(a, b, (((1,), (1,)), ((), ())), preferred_element_type=F32)


def nn_dot(a, b):
    return jnp.dot(a, b, preferred_element_type=F32)


def start_kernel(*refs):
    refs[-1][...] = jnp.zeros_like(refs[-1])


def forward_part(moment, drop, x, ra, rb, win, wout, gain, h, nrm, act, slp, sa, sb):
    section = lax.axis_index("section")
    count = ra.shape[0]
    chunk = moment - LAG * section
    per_sample = x.shape[0] // drop.shape[1] // count

    @pl.when(jnp.logical_and(chunk >= 0, chunk < CHUNKS))
    def _():
        rows = pl.ds(pl.multiple_of(chunk * count, count), count)

        @pl.when(section == 0)
        def _():
            h[rows, :] = x[rows, :]

        @pl.when(section % 2 == 1)
        def _():
            h[rows, :] = ra[...]

        @pl.when(section == 2)
        def _():
            h[rows, :] = rb[...]

        hf = h[rows, :].astype(F32)
        inv = lax.rsqrt(jnp.mean(hf * hf, axis=-1, keepdims=True) + EPSILON)
        normed = (hf * inv * gain[...].astype(F32)).astype(BF)
        nrm[rows, :] = normed
        total = jnp.zeros(hf.shape, F32)
        for at in range(0, win.shape[1], TILE):
            hid = nn_dot(normed, win[:, at : at + TILE])
            half = 0.5 * (1.0 + lax.erf(hid * ROOT_HALF))
            active = (hid * half).astype(BF)
            act[rows, at : at + TILE] = active
            slope = half + hid * jnp.exp(-0.5 * hid * hid) * DENSITY_SCALE
            slp[rows, at : at + TILE] = slope.astype(BF)
            total = total + nt_dot(active, wout[:, at : at + TILE])
        keep = drop[0, chunk // per_sample, 0, section].astype(F32)
        out = (hf + keep * total).astype(BF)

        @pl.when(section % 2 == 0)
        def _():
            sa[...] = out

        @pl.when(section % 2 == 1)
        def _():
            sb[...] = out


def backward_part(moment, drop, cot, ra, rb, win, wout, gain, h, slp, gat, ghd, gsum, sa, sb):
    section = lax.axis_index("section")
    count = ra.shape[0]
    chunk = moment - LAG * (2 * (STAGES - 1) - section)
    per_sample = cot.shape[0] // drop.shape[1] // count

    @pl.when(jnp.logical_and(chunk >= 0, chunk < CHUNKS))
    def _():
        rows = pl.ds(pl.multiple_of(chunk * count, count), count)

        @pl.when(section == STAGES - 1)
        def _():
            gat[rows, :] = cot[rows, :]

        @pl.when(section % 2 == 0)
        def _():
            gat[rows, :] = ra[...]

        @pl.when(section == 1)
        def _():
            gat[rows, :] = rb[...]

        up = gat[rows, :].astype(F32)
        keep = drop[0, chunk // per_sample, 0, section].astype(F32)
        gated = (keep * up).astype(BF)
        gat[rows, :] = gated
        total = jnp.zeros(up.shape, F32)
        for at in range(0, win.shape[1], TILE):
            grad_active = nn_dot(gated, wout[:, at : at + TILE])
            grad_hidden = (grad_active * slp[rows, at : at + TILE].astype(F32)).astype(BF)
            ghd[rows, at : at + TILE] = grad_hidden
            total = total + nt_dot(grad_hidden, win[:, at : at + TILE])
        hf = h[rows, :].astype(F32)
        inv = lax.rsqrt(jnp.mean(hf * hf, axis=-1, keepdims=True) + EPSILON)
        gsum[0:1, :] += jnp.sum(total * hf * inv, axis=0, keepdims=True)
        scaled = total * gain[...].astype(F32)
        centre = jnp.mean(scaled * hf, axis=-1, keepdims=True)
        out = (up + inv * (scaled - hf * inv * inv * centre)).astype(BF)

        @pl.when(section % 2 == 0)
        def _():
            sb[...] = out

        @pl.when(section % 2 == 1)
        def _():
            sa[...] = out


def slot_kernel(moment, has_f, has_b):
    def kernel(drop, x, cot, ra, rb, win, wout, gain, *rest):
        h, nrm, act, slp, gat, ghd, gsum, sa, sb = rest[7:]
        if has_f:
            forward_part(moment, drop, x, ra, rb, win, wout, gain, h, nrm, act, slp, sa, sb)
        if has_b:
            backward_part(moment, drop, cot, ra, rb, win, wout, gain, h, slp, gat, ghd, gsum, sa, sb)

    return kernel


def row_table(parts, width):
    each = width // parts
    table = np.zeros((2, parts, width), np.int32)
    for d in range(parts):
        c, x, y = d % 2, (d // 2) % SIDE_X, d // (2 * SIDE_X)
        for order in range(2):
            at = 0
            for core in (1 - c, c):
                for outer in range(4):
                    for inner in range(4):
                        dx, dy = (outer, inner) if order == 0 else (inner, outer)
                        dest = (((y + dy) % SIDE_Y) * SIDE_X + (x + dx) % SIDE_X) * 2 + core
                        table[order, d, at : at + each] = dest * each + np.arange(each)
                        at += each
    return table


def weight_kernel(tab_x, tab_y, nrm, ghd, gat, act, gsum, send_x, keep_x, send_y, keep_y, lhs):
    d = lax.axis_index("dp")
    width = nrm.shape[1]
    half = width // 2
    hidden = act.shape[1]

    def select(tab):
        wanted = tab[pl.ds(d, 1), :]
        places = lax.broadcasted_iota(jnp.int32, (width, width), 0)
        return jnp.where(places == wanted, 1.0, 0.0).astype(BF)

    def take(pick, source):
        return lax.dot_general(pick, source, (((0,), (1,)), ((), ())), preferred_element_type=F32).astype(BF)

    pick = select(tab_x)
    lhs[...] = take(pick, nrm[...])
    sums = jnp.broadcast_to(gsum[0:1, :].astype(BF), (PAD, width))
    col = take(pick, sums)
    send_x[:, hidden:] = col[:half]
    keep_x[:, hidden:] = col[half:]
    for at in range(0, hidden, TILE):
        rhs = ghd[:, at : at + TILE]
        send_x[:, at : at + TILE] = nn_dot(lhs[:half, :], rhs).astype(BF)
        keep_x[:, at : at + TILE] = nn_dot(lhs[half:, :], rhs).astype(BF)
    lhs[...] = take(select(tab_y), gat[...])
    for at in range(0, hidden, TILE):
        rhs = act[:, at : at + TILE]
        send_y[:, at : at + TILE] = nn_dot(lhs[:half, :], rhs).astype(BF)
        keep_y[:, at : at + TILE] = nn_dot(lhs[half:, :], rhs).astype(BF)


def add(*terms):
    total = terms[0].astype(F32)
    for term in terms[1:]:
        total = total + term.astype(F32)
    return total


def fold_kernel(count):
    def kernel(*refs):
        ins, outs = refs[:4], refs[4:]
        for side in range(2):
            keep, got = ins[2 * side], ins[2 * side + 1]
            rest, far_up, far_down = outs[3 * side : 3 * side + 3]
            mid = keep.shape[1] // 2
            far = slice(2 * count, 3 * count)
            far_up[...] = add(keep[far, :mid], got[far, :mid]).astype(BF)
            far_down[...] = add(keep[far, mid:], got[far, mid:]).astype(BF)
            rest[: 2 * count, :] = add(keep[: 2 * count, :], got[: 2 * count, :]).astype(BF)
            rest[2 * count :, :] = add(keep[3 * count :, :], got[3 * count :, :]).astype(BF)

    return kernel


def relay_kernel(count):
    def kernel(*refs):
        ins, outs = refs[:6], refs[6:]
        for side in range(2):
            rest, from_below, from_above = ins[3 * side : 3 * side + 3]
            up, down = outs[2 * side : 2 * side + 2]
            mid = rest.shape[1] // 2
            first, last = slice(count, 2 * count), slice(2 * count, 3 * count)
            up[:, :mid] = add(rest[first, :mid], from_below[...]).astype(BF)
            up[:, mid:] = rest[first, mid:].astype(BF)
            down[:, :mid] = rest[last, :mid].astype(BF)
            down[:, mid:] = add(rest[last, mid:], from_above[...]).astype(BF)

    return kernel


def turn_kernel(count):
    each = count // 4

    def kernel(*refs):
        ins, outs = refs[:6], refs[6:]
        for side in range(2):
            rest, from_below, from_above = ins[3 * side : 3 * side + 3]
            left, far_up, far_down = outs[3 * side : 3 * side + 3]
            mid = rest.shape[1] // 2
            total = add(rest[:count, :], from_below[...], from_above[...])
            far_up[...] = total[2 * each : 3 * each, :mid].astype(BF)
            far_down[...] = total[2 * each : 3 * each, mid:].astype(BF)
            left[: 2 * each, :] = total[: 2 * each, :]
            left[2 * each :, :] = total[3 * each :, :]

    return kernel


def final_kernel(left_x, up_x, down_x, left_y, up_y, down_y, out_in, out_out, out_gain):
    each, hidden = out_in.shape
    total = add(left_x[:each, :], up_x[...], down_x[...])
    out_in[...] = total[:, :hidden]
    out_gain[...] = total[:, hidden:]
    out_out[...] = add(left_y[:each, :], up_y[...], down_y[...])


def per_device(x_in, cotangent, w_in, w_out, gain, drop_mask):
    parts = lax.axis_size("dp")
    width, hidden = w_in.shape[1], w_in.shape[2]
    x = x_in.reshape(-1, width)
    cot = cotangent.reshape(-1, width)
    rows = x.shape[0]
    count = rows // CHUNKS
    win, wout = w_in[0], w_out[0]
    shapes = [
        ((rows, width), BF),
        ((rows, width), BF),
        ((rows, hidden), BF),
        ((rows, hidden), BF),
        ((rows, width), BF),
        ((rows, hidden), BF),
        ((8, width), F32),
    ]
    state = vmem_call(start_kernel, shapes, ())
    low_pairs = [(0, 1), (1, 0), (2, 3), (3, 2)]
    high_pairs = [(1, 2), (2, 1), (3, 0), (0, 3)]
    sent_a, sent_b = {}, {}
    blank = x[:count]
    turn = LAG * (STAGES - 1)
    for moment in range(CHUNKS + 2 * turn):
        has_f = moment < CHUNKS + turn
        has_b = moment >= turn
        ra = sent_a.get(moment - LAG, blank)
        rb = sent_b.get(moment - LAG, blank)
        work = 4 * count * width * hidden
        found = vmem_call(
            slot_kernel(moment, has_f, has_b),
            shapes + [((count, width), BF), ((count, width), BF)],
            (drop_mask, x, cot, ra, rb, win, wout, gain, *state),
            specs=[SMEM_SPEC] + [VMEM_SPEC] * 14,
            aliases={8 + i: i for i in range(7)},
            flops=work * (int(has_f) + int(has_b)),
            moved=4 * width * hidden,
        )
        state = found[:7]
        if moment < CHUNKS + 2 * turn - LAG:
            sent_a[moment] = lax.ppermute(found[7], "section", low_pairs)
            if LAG <= moment < CHUNKS + 2 * turn - 2 * LAG:
                sent_b[moment] = lax.ppermute(found[8], "section", high_pairs)
    h, nrm, act, slp, gat, ghd, gsum = state

    table = row_table(parts, width)
    half = width // 2
    wide = hidden + PAD
    send_x, keep_x, send_y, keep_y = vmem_call(
        weight_kernel,
        [((half, wide), BF), ((half, wide), BF), ((half, hidden), BF), ((half, hidden), BF)],
        (jnp.asarray(table[0]), jnp.asarray(table[1]), nrm, ghd, gat, act, gsum),
        scratch=[pltpu.VMEM((width, rows), BF)],
        limit=20,
        flops=4 * rows * width * hidden,
        moved=4 * width * hidden,
    )

    def place(d):
        return d // (2 * SIDE_X), (d // 2) % SIDE_X, d % 2

    def index(y, x, c):
        return ((y % SIDE_Y) * SIDE_X + x % SIDE_X) * 2 + c

    def route(dy, dx, flip=0):
        return [(d, index(place(d)[0] + dy, place(d)[1] + dx, place(d)[2] ^ flip)) for d in range(parts)]

    def go(block, *step):
        return lax.ppermute(block, "dp", route(*step))

    got_x = go(send_x, 0, 0, 1)
    got_y = go(send_y, 0, 0, 1)
    count = half // 4
    each = count // 4
    rest_x, fu_x, fd_x, rest_y, fu_y, fd_y = vmem_call(
        fold_kernel(count),
        [((3 * count, wide), BF)] + [((count, wide // 2), BF)] * 2
        + [((3 * count, hidden), BF)] + [((count, hidden // 2), BF)] * 2,
        (keep_x, got_x, keep_y, got_y),
    )
    up_x, down_x, up_y, down_y = vmem_call(
        relay_kernel(count),
        [((count, wide), BF)] * 2 + [((count, hidden), BF)] * 2,
        (rest_x, go(fu_x, 0, 1), go(fd_x, 0, -1), rest_y, go(fu_y, 1, 0), go(fd_y, -1, 0)),
    )
    left_x, fu_x, fd_x, left_y, fu_y, fd_y = vmem_call(
        turn_kernel(count),
        [((3 * each, wide), F32)] + [((each, wide // 2), BF)] * 2
        + [((3 * each, hidden), F32)] + [((each, hidden // 2), BF)] * 2,
        (rest_x, go(up_x, 0, 1), go(down_x, 0, -1), rest_y, go(up_y, 1, 0), go(down_y, -1, 0)),
    )
    up_x, down_x, up_y, down_y = vmem_call(
        relay_kernel(each),
        [((each, wide), BF)] * 2 + [((each, hidden), BF)] * 2,
        (left_x, go(fu_x, 1, 0), go(fd_x, -1, 0), left_y, go(fu_y, 0, 1), go(fd_y, 0, -1)),
    )
    out_in, out_out, out_gain = pl.pallas_call(
        final_kernel,
        out_shape=(
            jax.ShapeDtypeStruct((each, hidden), F32),
            jax.ShapeDtypeStruct((each, hidden), F32),
            jax.ShapeDtypeStruct((each, PAD), F32),
        ),
        in_specs=[VMEM_SPEC] * 6,
        out_specs=(VMEM_SPEC,) * 3,
        compiler_params=pltpu.CompilerParams(vmem_limit_bytes=16 * MIB),
    )(left_x, go(up_x, 1, 0), go(down_x, -1, 0), left_y, go(up_y, 0, 1), go(down_y, 0, -1))
    return out_in[None], out_out[None], out_gain[:, 0][None]


def solution(mesh):
    placed = (
        P("dp", None, None, None),
        P("dp", None, None, None),
        P("section", None, None),
        P("section", None, None),
        P("section", None),
        P("dp", None, None, None),
    )
    return jax.shard_map(
        per_device,
        mesh=mesh,
        in_specs=placed,
        out_specs=(P("section", "dp", None), P("section", "dp", None), P("section", "dp")),
        check_vma=False,
    )
```

```python
import jax
import jax.numpy as jnp
import numpy as np
from jax import lax
from jax.experimental import pallas as pl
from jax.experimental.pallas import tpu as pltpu
from jax.sharding import PartitionSpec as P


EPSILON = 1e-05
ROOT_HALF = 0.7071067811865476
DENSITY_SCALE = 0.3989422804014327
BF = jnp.bfloat16
F32 = jnp.float32
STAGES = 4
LAG = 2
CHUNKS = 4
TILE = 512
WIDE = 1024
PAD = 128
LOADS = 6
SIDE_X = 4
SIDE_Y = 4
MIB = 1024 * 1024

VMEM_SPEC = pl.BlockSpec(memory_space=pltpu.VMEM)
SMEM_SPEC = pl.BlockSpec(memory_space=pltpu.SMEM)


def vmem_call(kernel, outs, args, specs=None, aliases=None, limit=16, flops=0, moved=0, scratch=()):
    return pl.pallas_call(
        kernel,
        out_shape=tuple(pltpu.VMEM(shape, dtype) for shape, dtype in outs),
        in_specs=specs or [VMEM_SPEC] * len(args),
        out_specs=tuple(VMEM_SPEC for _ in outs),
        input_output_aliases=aliases or {},
        scratch_shapes=list(scratch),
        compiler_params=pltpu.CompilerParams(vmem_limit_bytes=limit * MIB),
        cost_estimate=pl.CostEstimate(flops=flops, bytes_accessed=moved, transcendentals=0),
    )(*args)


def nn_dot(a, b):
    return jnp.dot(a, b, preferred_element_type=F32)


def start_kernel(drop_in, x, cot, win_in, wout_in, gain_in, *refs):
    keeps, win, wout, win_t, wout_t, gain, blank, h, nrm, act, slp, gat, ghd, gsum, drop, sems, own = refs
    section = lax.axis_index("section")
    hidden = win.shape[1]
    tiles = range(0, hidden, hidden // LOADS)

    def piece(source, target, at, sem):
        cols = pl.ds(at, hidden // LOADS)
        return pltpu.make_async_copy(source.at[:, cols], target.at[:, cols], sem)

    copies = [
        (piece(win_in, win, at, sems.at[0, i]), piece(wout_in, wout, at, sems.at[1, i])) for i, at in enumerate(tiles)
    ]
    marks = pltpu.make_async_copy(drop_in, drop, own.at[0])
    scale = pltpu.make_async_copy(gain_in, gain, own.at[1])
    first = pltpu.make_async_copy(x, h, own.at[2])
    last = pltpu.make_async_copy(cot, gat, own.at[2])
    marks.start()
    scale.start()
    for both in copies:
        both[0].start()
        both[1].start()

    @pl.when(section == 0)
    def _():
        first.start()

    @pl.when(section == STAGES - 1)
    def _():
        last.start()

    gsum[...] = jnp.zeros_like(gsum)
    marks.wait()
    for chunk in range(CHUNKS):
        mark = drop[0, chunk * drop_in.shape[1] // CHUNKS, 0, section].astype(F32)
        keeps[chunk : chunk + 1, :] = jnp.full((1, keeps.shape[1]), mark, F32)
    for i, at in enumerate(tiles):
        size = hidden // LOADS
        copies[i][0].wait()
        win_t[at : at + size, :] = win[:, at : at + size].T
        copies[i][1].wait()
        wout_t[at : at + size, :] = wout[:, at : at + size].T
    scale.wait()

    @pl.when(section == 0)
    def _():
        first.wait()

    @pl.when(section == STAGES - 1)
    def _():
        last.wait()


def forward_part(moment, keeps, ra, rb, win, wout_t, gain, h, nrm, act, slp, sa, sb):
    section = lax.axis_index("section")
    count = ra.shape[0]
    chunk = moment - LAG * section

    @pl.when(jnp.logical_and(chunk >= 0, chunk < CHUNKS))
    def _():
        rows = pl.ds(pl.multiple_of(chunk * count, count), count)

        @pl.when(section % 2 == 1)
        def _():
            h[rows, :] = ra[...]

        @pl.when(section == 2)
        def _():
            h[rows, :] = rb[...]

        hf = h[rows, :].astype(F32)
        inv = lax.rsqrt(jnp.mean(hf * hf, axis=-1, keepdims=True) + EPSILON)
        normed = (hf * inv * gain[...].astype(F32)).astype(BF)
        nrm[rows, :] = normed
        for at in range(0, win.shape[1], TILE):
            hid = nn_dot(normed, win[:, at : at + TILE])
            half = 0.5 * (1.0 + lax.erf(hid * ROOT_HALF))
            active = (hid * half).astype(BF)
            act[rows, at : at + TILE] = active
            slope = half + hid * jnp.exp(-0.5 * hid * hid) * DENSITY_SCALE
            slp[rows, at : at + TILE] = slope.astype(BF)
        total = nn_dot(act[rows, :], wout_t[...])
        keep = keeps[pl.ds(chunk, 1), :][:, 0:1]
        out = (hf + keep * total).astype(BF)

        @pl.when(section % 2 == 0)
        def _():
            sa[...] = out

        @pl.when(section % 2 == 1)
        def _():
            sb[...] = out


def backward_part(moment, keeps, ra, rb, win_t, wout, gain, h, slp, gat, ghd, gsum, sa, sb):
    section = lax.axis_index("section")
    count = ra.shape[0]
    chunk = moment - LAG * (2 * (STAGES - 1) - section)

    @pl.when(jnp.logical_and(chunk >= 0, chunk < CHUNKS))
    def _():
        rows = pl.ds(pl.multiple_of(chunk * count, count), count)

        @pl.when(section % 2 == 0)
        def _():
            gat[rows, :] = ra[...]

        @pl.when(section == 1)
        def _():
            gat[rows, :] = rb[...]

        up = gat[rows, :].astype(F32)
        keep = keeps[pl.ds(chunk, 1), :][:, 0:1]
        gated = (keep * up).astype(BF)
        gat[rows, :] = gated
        for at in range(0, wout.shape[1], TILE):
            grad_active = nn_dot(gated, wout[:, at : at + TILE])
            grad_hidden = (grad_active * slp[rows, at : at + TILE].astype(F32)).astype(BF)
            ghd[rows, at : at + TILE] = grad_hidden
        total = nn_dot(ghd[rows, :], win_t[...])
        hf = h[rows, :].astype(F32)
        inv = lax.rsqrt(jnp.mean(hf * hf, axis=-1, keepdims=True) + EPSILON)
        gsum[0:1, :] += jnp.sum(total * hf * inv, axis=0, keepdims=True)
        scaled = total * gain[...].astype(F32)
        centre = jnp.mean(scaled * hf, axis=-1, keepdims=True)
        out = (up + inv * (scaled - hf * inv * inv * centre)).astype(BF)

        @pl.when(section % 2 == 0)
        def _():
            sb[...] = out

        @pl.when(section % 2 == 1)
        def _():
            sa[...] = out


def slot_kernel(moment, has_f, has_b):
    def kernel(keeps, ra, rb, win, wout, win_t, wout_t, gain, *rest):
        h, nrm, act, slp, gat, ghd, gsum, sa, sb = rest[7:]
        if has_f:
            forward_part(moment, keeps, ra, rb, win, wout_t, gain, h, nrm, act, slp, sa, sb)
        if has_b:
            backward_part(moment, keeps, ra, rb, win_t, wout, gain, h, slp, gat, ghd, gsum, sa, sb)

    return kernel


def row_table(parts, width):
    each = width // parts
    table = np.zeros((2, parts, width), np.int32)
    for d in range(parts):
        c, x, y = d % 2, (d // 2) % SIDE_X, d // (2 * SIDE_X)
        for order in range(2):
            at = 0
            for core in (1 - c, c):
                for outer in range(4):
                    for inner in range(4):
                        dx, dy = (outer, inner) if order == 0 else (inner, outer)
                        dest = (((y + dy) % SIDE_Y) * SIDE_X + (x + dx) % SIDE_X) * 2 + core
                        table[order, d, at : at + each] = dest * each + np.arange(each)
                        at += each
    return table


def weight_kernel(tab, left, right, *rest):
    *sums, send, keep, lhs = rest
    d = lax.axis_index("dp")
    width = left.shape[1]
    half = width // 2
    hidden = right.shape[1]
    wanted = tab[pl.ds(d, 1), :]
    places = lax.broadcasted_iota(jnp.int32, (width, width), 0)
    pick = jnp.where(places == wanted, 1.0, 0.0).astype(BF)

    def take(source):
        return lax.dot_general(pick, source, (((0,), (1,)), ((), ())), preferred_element_type=F32).astype(BF)

    lhs[...] = take(left[...])
    if sums:
        col = take(jnp.broadcast_to(sums[0][0:1, :].astype(BF), (PAD, width)))
        send[:, hidden:] = col[:half]
        keep[:, hidden:] = col[half:]

    @pl.loop(0, hidden // WIDE)
    def _(step):
        cols = pl.ds(pl.multiple_of(step * WIDE, WIDE), WIDE)
        send[:, cols] = nn_dot(lhs[:half, :], right[:, cols]).astype(BF)
        keep[:, cols] = nn_dot(lhs[half:, :], right[:, cols]).astype(BF)


def add(*terms):
    total = terms[0].astype(F32)
    for term in terms[1:]:
        total = total + term.astype(F32)
    return total


def far_kernel(keep, got, far_up, far_down):
    count = far_up.shape[0]
    mid = keep.shape[1] // 2
    far = slice(2 * count, 3 * count)
    far_up[...] = add(keep[far, :mid], got[far, :mid]).astype(BF)
    far_down[...] = add(keep[far, mid:], got[far, mid:]).astype(BF)


def rest_kernel(keep, got, rest):
    count = keep.shape[0] // 4
    rest[: 2 * count, :] = add(keep[: 2 * count, :], got[: 2 * count, :]).astype(BF)
    rest[2 * count :, :] = add(keep[3 * count :, :], got[3 * count :, :]).astype(BF)


def relay_kernel(rest, from_below, from_above, up, down):
    count = up.shape[0]
    mid = rest.shape[1] // 2
    first, last = slice(count, 2 * count), slice(2 * count, 3 * count)
    up[:, :mid] = add(rest[first, :mid], from_below[...]).astype(BF)
    up[:, mid:] = rest[first, mid:].astype(BF)
    down[:, :mid] = rest[last, :mid].astype(BF)
    down[:, mid:] = add(rest[last, mid:], from_above[...]).astype(BF)


def turn_kernel(rest, from_below, from_above, own, *others):
    count = from_below.shape[0]
    each = count // 4
    total = add(rest[:count, :], from_below[...], from_above[...])
    own[...] = total[:each, :]
    for place, other in enumerate(others, 1):
        other[...] = total[place * each : (place + 1) * each, :].astype(BF)


def final_kernel(own, one, two, three, out, *gains):
    each, hidden = out.shape
    total = add(own[...], one[...], two[...], three[...])
    out[...] = total[:, :hidden]
    if gains:
        places = lax.broadcasted_iota(jnp.int32, (each, PAD), 0)
        lanes = lax.broadcasted_iota(jnp.int32, (each, PAD), 1)
        line = jnp.sum(jnp.where(places == lanes, total[:, hidden:], 0.0), axis=0, keepdims=True)
        gains[0][...] = line[:, :each]


def per_device(x_in, cotangent, w_in, w_out, gain, drop_mask):
    parts = lax.axis_size("dp")
    width, hidden = w_in.shape[1], w_in.shape[2]
    x = x_in.reshape(-1, width)
    cot = cotangent.reshape(-1, width)
    rows = x.shape[0]
    count = rows // CHUNKS
    shapes = [
        ((rows, width), BF),
        ((rows, width), BF),
        ((rows, hidden), BF),
        ((rows, hidden), BF),
        ((rows, width), BF),
        ((rows, hidden), BF),
        ((8, width), F32),
    ]
    keeps, win, wout, win_t, wout_t, scale, blank, *state = vmem_call(
        start_kernel,
        [((8, 128), F32)]
        + [((width, hidden), BF)] * 2
        + [((hidden, width), BF)] * 2
        + [((1, width), BF), ((count, width), BF)]
        + shapes,
        tuple(pltpu.with_memory_space_constraint(a, pltpu.HBM) for a in (drop_mask, x, cot, w_in[0], w_out[0], gain)),
        specs=[pl.BlockSpec(memory_space=pltpu.HBM)] * 6,
        scratch=[
            pltpu.SMEM(drop_mask.shape, drop_mask.dtype),
            pltpu.SemaphoreType.DMA((2, LOADS)),
            pltpu.SemaphoreType.DMA((3,)),
        ],
    )
    low_pairs = [(0, 1), (1, 0), (2, 3), (3, 2)]
    high_pairs = [(1, 2), (2, 1), (3, 0), (0, 3)]
    sent_a, sent_b = {}, {}
    turn = LAG * (STAGES - 1)
    for moment in range(CHUNKS + 2 * turn):
        has_f = moment < CHUNKS + turn
        has_b = moment >= turn
        ra = sent_a.get(moment - LAG, blank)
        rb = sent_b.get(moment - LAG, blank)
        work = 4 * count * width * hidden
        found = vmem_call(
            slot_kernel(moment, has_f, has_b),
            shapes + [((count, width), BF), ((count, width), BF)],
            (keeps, ra, rb, win, wout, win_t, wout_t, scale, *state),
            aliases={8 + i: i for i in range(7)},
            flops=work * (int(has_f) + int(has_b)),
            moved=4 * width * hidden,
        )
        state = found[:7]
        if moment < CHUNKS + 2 * turn - LAG:
            sent_a[moment] = lax.ppermute(found[7], "section", low_pairs)
            if LAG <= moment < CHUNKS + 2 * turn - 2 * LAG:
                sent_b[moment] = lax.ppermute(found[8], "section", high_pairs)
    h, nrm, act, slp, gat, ghd, gsum = state

    table = row_table(parts, width)
    half = width // 2

    def place(d):
        return d // (2 * SIDE_X), (d // 2) % SIDE_X, d % 2

    def index(y, x, c):
        return ((y % SIDE_Y) * SIDE_X + x % SIDE_X) * 2 + c

    def go(block, dy, dx, flip=0):
        route = [(d, index(place(d)[0] + dy, place(d)[1] + dx, place(d)[2] ^ flip)) for d in range(parts)]
        return lax.ppermute(block, "dp", route)

    def gradient(tab, left, right, sums):
        wide = hidden + (PAD if sums else 0)
        send, keep = vmem_call(
            weight_kernel,
            [((half, wide), BF)] * 2,
            (jnp.asarray(tab), left, right, *sums),
            scratch=[pltpu.VMEM((width, rows), BF)],
            flops=2 * rows * width * hidden,
            moved=2 * width * hidden,
        )
        return keep, go(send, 0, 0, 1)

    def ring(pair, first, second):
        keep, got = pair
        wide = keep.shape[1]
        line = half // 4
        far = vmem_call(far_kernel, [((line, wide // 2), BF)] * 2, (keep, got))
        (rest,) = vmem_call(rest_kernel, [((3 * line, wide), BF)], (keep, got))
        below, above = go(far[0], *first), go(far[1], -first[0], -first[1])
        up, down = vmem_call(relay_kernel, [((line, wide), BF)] * 2, (rest, below, above))
        below, above = go(up, *first), go(down, -first[0], -first[1])
        each = line // 4
        own, *others = vmem_call(
            turn_kernel,
            [((each, wide), F32)] + [((each, wide), BF)] * 3,
            (rest, below, above),
        )
        found = [go(others[k - 1], k * second[0], k * second[1]) for k in (2, 1, 3)]
        shapes = [jax.ShapeDtypeStruct((each, hidden), F32)]
        if wide > hidden:
            shapes.append(jax.ShapeDtypeStruct((1, each), F32))
        return pl.pallas_call(
            final_kernel,
            out_shape=tuple(shapes),
            in_specs=[VMEM_SPEC] * 4,
            out_specs=(VMEM_SPEC,) * len(shapes),
            compiler_params=pltpu.CompilerParams(vmem_limit_bytes=16 * MIB),
        )(own, *found)

    pair_y = gradient(table[1], gat, act, ())
    pair_x = gradient(table[0], nrm, ghd, (gsum,))
    (out_out,) = ring(pair_y, (1, 0), (0, 1))
    out_in, out_gain = ring(pair_x, (0, 1), (1, 0))
    return out_in[None], out_out[None], out_gain


def solution(mesh):
    placed = (
        P("dp", None, None, None),
        P("dp", None, None, None),
        P("section", None, None),
        P("section", None, None),
        P("section", None),
        P("dp", None, None, None),
    )
    return jax.shard_map(
        per_device,
        mesh=mesh,
        in_specs=placed,
        out_specs=(P("section", "dp", None), P("section", "dp", None), P("section", "dp")),
        check_vma=False,
    )
```

```python
import jax
import jax.numpy as jnp
import numpy as np
from jax import lax
from jax.experimental import pallas as pl
from jax.experimental.pallas import tpu as pltpu
from jax.sharding import PartitionSpec as P


EPSILON = 1e-05
ROOT_HALF = 0.7071067811865476
DENSITY_SCALE = 0.3989422804014327
BF = jnp.bfloat16
F32 = jnp.float32
STAGES = 4
LAG = 2
CHUNKS = 4
TILE = 512
WIDE = 1024
PAD = 128
LOADS = 6
SIDE_X = 4
SIDE_Y = 4
MIB = 1024 * 1024

VMEM_SPEC = pl.BlockSpec(memory_space=pltpu.VMEM)
SMEM_SPEC = pl.BlockSpec(memory_space=pltpu.SMEM)


def vmem_call(kernel, outs, args, specs=None, aliases=None, limit=16, flops=0, moved=0, scratch=()):
    return pl.pallas_call(
        kernel,
        out_shape=tuple(pltpu.VMEM(shape, dtype) for shape, dtype in outs),
        in_specs=specs or [VMEM_SPEC] * len(args),
        out_specs=tuple(VMEM_SPEC for _ in outs),
        input_output_aliases=aliases or {},
        scratch_shapes=list(scratch),
        compiler_params=pltpu.CompilerParams(vmem_limit_bytes=limit * MIB),
        cost_estimate=pl.CostEstimate(flops=flops, bytes_accessed=moved, transcendentals=0),
    )(*args)


def nn_dot(a, b):
    return jnp.dot(a, b, preferred_element_type=F32)


def start_kernel(drop_in, x, cot, win_in, wout_in, gain_in, *refs):
    keeps, win, wout, win_t, wout_t, gain, blank, h, nrm, act, slp, gat, ghd, gsum, drop, sems, own = refs
    section = lax.axis_index("section")
    hidden = win.shape[1]
    tiles = range(0, hidden, hidden // LOADS)

    def piece(source, target, at, sem):
        cols = pl.ds(at, hidden // LOADS)
        return pltpu.make_async_copy(source.at[:, cols], target.at[:, cols], sem)

    copies = [
        (piece(win_in, win, at, sems.at[0, i]), piece(wout_in, wout, at, sems.at[1, i])) for i, at in enumerate(tiles)
    ]
    marks = pltpu.make_async_copy(drop_in, drop, own.at[0])
    scale = pltpu.make_async_copy(gain_in, gain, own.at[1])
    first = pltpu.make_async_copy(x, h, own.at[2])
    last = pltpu.make_async_copy(cot, gat, own.at[2])
    marks.start()
    scale.start()
    for both in copies:
        both[0].start()
        both[1].start()

    @pl.when(section == 0)
    def _():
        first.start()

    @pl.when(section == STAGES - 1)
    def _():
        last.start()

    gsum[...] = jnp.zeros_like(gsum)
    marks.wait()
    for chunk in range(CHUNKS):
        mark = drop[0, chunk * drop_in.shape[1] // CHUNKS, 0, section].astype(F32)
        keeps[chunk : chunk + 1, :] = jnp.full((1, keeps.shape[1]), mark, F32)
    for i, at in enumerate(tiles):
        size = hidden // LOADS
        copies[i][0].wait()
        win_t[at : at + size, :] = win[:, at : at + size].T
        copies[i][1].wait()
        wout_t[at : at + size, :] = wout[:, at : at + size].T
    scale.wait()

    @pl.when(section == 0)
    def _():
        first.wait()

    @pl.when(section == STAGES - 1)
    def _():
        last.wait()


def forward_part(moment, keeps, ra, rb, win, wout_t, gain, h, nrm, act, slp, sa, sb):
    section = lax.axis_index("section")
    count = ra.shape[0]
    chunk = moment - LAG * section

    @pl.when(jnp.logical_and(chunk >= 0, chunk < CHUNKS))
    def _():
        rows = pl.ds(pl.multiple_of(chunk * count, count), count)

        @pl.when(section % 2 == 1)
        def _():
            h[rows, :] = ra[...]

        @pl.when(section == 2)
        def _():
            h[rows, :] = rb[...]

        hf = h[rows, :].astype(F32)
        inv = lax.rsqrt(jnp.mean(hf * hf, axis=-1, keepdims=True) + EPSILON)
        normed = (hf * inv * gain[...].astype(F32)).astype(BF)
        nrm[rows, :] = normed
        for at in range(0, win.shape[1], TILE):
            hid = nn_dot(normed, win[:, at : at + TILE])
            half = 0.5 * (1.0 + lax.erf(hid * ROOT_HALF))
            active = (hid * half).astype(BF)
            act[rows, at : at + TILE] = active
            slope = half + hid * jnp.exp(-0.5 * hid * hid) * DENSITY_SCALE
            slp[rows, at : at + TILE] = slope.astype(BF)
        total = nn_dot(act[rows, :], wout_t[...])
        keep = keeps[pl.ds(chunk, 1), :][:, 0:1]
        out = (hf + keep * total).astype(BF)

        @pl.when(section % 2 == 0)
        def _():
            sa[...] = out

        @pl.when(section % 2 == 1)
        def _():
            sb[...] = out


def backward_part(moment, keeps, ra, rb, win_t, wout, gain, h, slp, gat, ghd, gsum, sa, sb):
    section = lax.axis_index("section")
    count = ra.shape[0]
    chunk = moment - LAG * (2 * (STAGES - 1) - section)

    @pl.when(jnp.logical_and(chunk >= 0, chunk < CHUNKS))
    def _():
        rows = pl.ds(pl.multiple_of(chunk * count, count), count)

        @pl.when(section % 2 == 0)
        def _():
            gat[rows, :] = ra[...]

        @pl.when(section == 1)
        def _():
            gat[rows, :] = rb[...]

        up = gat[rows, :].astype(F32)
        keep = keeps[pl.ds(chunk, 1), :][:, 0:1]
        gated = (keep * up).astype(BF)
        gat[rows, :] = gated
        for at in range(0, wout.shape[1], TILE):
            grad_active = nn_dot(gated, wout[:, at : at + TILE])
            grad_hidden = (grad_active * slp[rows, at : at + TILE].astype(F32)).astype(BF)
            ghd[rows, at : at + TILE] = grad_hidden
        total = nn_dot(ghd[rows, :], win_t[...])
        hf = h[rows, :].astype(F32)
        inv = lax.rsqrt(jnp.mean(hf * hf, axis=-1, keepdims=True) + EPSILON)
        gsum[0:1, :] += jnp.sum(total * hf * inv, axis=0, keepdims=True)
        scaled = total * gain[...].astype(F32)
        centre = jnp.mean(scaled * hf, axis=-1, keepdims=True)
        out = (up + inv * (scaled - hf * inv * inv * centre)).astype(BF)

        @pl.when(section % 2 == 0)
        def _():
            sb[...] = out

        @pl.when(section % 2 == 1)
        def _():
            sa[...] = out


def slot_kernel(moment, has_f, has_b):
    def kernel(keeps, ra, rb, win, wout, win_t, wout_t, gain, *rest):
        h, nrm, act, slp, gat, ghd, gsum, sa, sb = rest[7:]
        if has_f:
            forward_part(moment, keeps, ra, rb, win, wout_t, gain, h, nrm, act, slp, sa, sb)
        if has_b:
            backward_part(moment, keeps, ra, rb, win_t, wout, gain, h, slp, gat, ghd, gsum, sa, sb)

    return kernel


def row_table(parts, width):
    each = width // parts
    table = np.zeros((2, parts, width), np.int32)
    for d in range(parts):
        c, x, y = d % 2, (d // 2) % SIDE_X, d // (2 * SIDE_X)
        for order in range(2):
            at = 0
            for core in (1 - c, c):
                for outer in range(4):
                    for inner in range(4):
                        dx, dy = (outer, inner) if order == 0 else (inner, outer)
                        dest = (((y + dy) % SIDE_Y) * SIDE_X + (x + dx) % SIDE_X) * 2 + core
                        table[order, d, at : at + each] = dest * each + np.arange(each)
                        at += each
    return table


def weight_kernel(tab, left, right, *rest):
    *sums, send, keep, lhs = rest
    d = lax.axis_index("dp")
    width = left.shape[1]
    half = width // 2
    hidden = right.shape[1]
    wanted = tab[pl.ds(d, 1), :]
    places = lax.broadcasted_iota(jnp.int32, (width, width), 0)
    pick = jnp.where(places == wanted, 1.0, 0.0).astype(BF)

    def take(source):
        return lax.dot_general(pick, source, (((0,), (1,)), ((), ())), preferred_element_type=F32).astype(BF)

    lhs[...] = take(left[...])
    if sums:
        col = take(jnp.broadcast_to(sums[0][0:1, :].astype(BF), (PAD, width)))
        send[:, hidden:] = col[:half]
        keep[:, hidden:] = col[half:]

    @pl.loop(0, hidden // WIDE)
    def _(step):
        cols = pl.ds(pl.multiple_of(step * WIDE, WIDE), WIDE)
        send[:, cols] = nn_dot(lhs[:half, :], right[:, cols]).astype(BF)
        keep[:, cols] = nn_dot(lhs[half:, :], right[:, cols]).astype(BF)


def add(*terms):
    total = terms[0].astype(F32)
    for term in terms[1:]:
        total = total + term.astype(F32)
    return total


def far_kernel(keep, got, far_up, far_down):
    count = far_up.shape[0]
    mid = keep.shape[1] // 2
    far = slice(2 * count, 3 * count)
    far_up[...] = add(keep[far, :mid], got[far, :mid]).astype(BF)
    far_down[...] = add(keep[far, mid:], got[far, mid:]).astype(BF)


def rest_kernel(keep, got, rest):
    count = keep.shape[0] // 4
    rest[: 2 * count, :] = add(keep[: 2 * count, :], got[: 2 * count, :]).astype(BF)
    rest[2 * count :, :] = add(keep[3 * count :, :], got[3 * count :, :]).astype(BF)


def relay_kernel(rest, from_below, from_above, up, down):
    count = up.shape[0]
    mid = rest.shape[1] // 2
    first, last = slice(count, 2 * count), slice(2 * count, 3 * count)
    up[:, :mid] = add(rest[first, :mid], from_below[...]).astype(BF)
    up[:, mid:] = rest[first, mid:].astype(BF)
    down[:, :mid] = rest[last, :mid].astype(BF)
    down[:, mid:] = add(rest[last, mid:], from_above[...]).astype(BF)


def turn_kernel(rest, from_below, from_above, own, *others):
    count = from_below.shape[0]
    each = count // 4
    total = add(rest[:count, :], from_below[...], from_above[...])
    own[...] = total[:each, :]
    for place, other in enumerate(others, 1):
        other[...] = total[place * each : (place + 1) * each, :].astype(BF)


def final_kernel(own, one, two, three, out, *gains):
    each, hidden = out.shape
    total = add(own[...], one[...], two[...], three[...])
    out[...] = total[:, :hidden]
    if gains:
        places = lax.broadcasted_iota(jnp.int32, (each, PAD), 0)
        lanes = lax.broadcasted_iota(jnp.int32, (each, PAD), 1)
        line = jnp.sum(jnp.where(places == lanes, total[:, hidden:], 0.0), axis=0, keepdims=True)
        gains[0][...] = line[:, :each]


def per_device(x_in, cotangent, w_in, w_out, gain, drop_mask):
    parts = lax.axis_size("dp")
    width, hidden = w_in.shape[1], w_in.shape[2]
    x = x_in.reshape(-1, width)
    cot = cotangent.reshape(-1, width)
    rows = x.shape[0]
    count = rows // CHUNKS
    shapes = [
        ((rows, width), BF),
        ((rows, width), BF),
        ((rows, hidden), BF),
        ((rows, hidden), BF),
        ((rows, width), BF),
        ((rows, hidden), BF),
        ((8, width), F32),
    ]
    keeps, win, wout, win_t, wout_t, scale, blank, *state = vmem_call(
        start_kernel,
        [((8, 128), F32)]
        + [((width, hidden), BF)] * 2
        + [((hidden, width), BF)] * 2
        + [((1, width), BF), ((count, width), BF)]
        + shapes,
        tuple(pltpu.with_memory_space_constraint(a, pltpu.HBM) for a in (drop_mask, x, cot, w_in[0], w_out[0], gain)),
        specs=[pl.BlockSpec(memory_space=pltpu.HBM)] * 6,
        scratch=[
            pltpu.SMEM(drop_mask.shape, drop_mask.dtype),
            pltpu.SemaphoreType.DMA((2, LOADS)),
            pltpu.SemaphoreType.DMA((3,)),
        ],
    )
    low_pairs = [(0, 1), (1, 0), (2, 3), (3, 2)]
    high_pairs = [(1, 2), (2, 1), (3, 0), (0, 3)]
    sent_a, sent_b = {}, {}
    turn = LAG * (STAGES - 1)
    for moment in range(CHUNKS + 2 * turn):
        has_f = moment < CHUNKS + turn
        has_b = moment >= turn
        ra = sent_a.get(moment - LAG, blank)
        rb = sent_b.get(moment - LAG, blank)
        work = 4 * count * width * hidden
        found = vmem_call(
            slot_kernel(moment, has_f, has_b),
            shapes + [((count, width), BF), ((count, width), BF)],
            (keeps, ra, rb, win, wout, win_t, wout_t, scale, *state),
            aliases={8 + i: i for i in range(7)},
            flops=work * (int(has_f) + int(has_b)),
            moved=4 * width * hidden,
        )
        state = found[:7]
        if moment < CHUNKS + 2 * turn - LAG:
            sent_a[moment] = lax.ppermute(found[7], "section", low_pairs)
            if LAG <= moment < CHUNKS + LAG or turn + LAG <= moment < CHUNKS + 2 * turn - 2 * LAG:
                sent_b[moment] = lax.ppermute(found[8], "section", high_pairs)
    h, nrm, act, slp, gat, ghd, gsum = state

    table = row_table(parts, width)
    half = width // 2

    def place(d):
        return d // (2 * SIDE_X), (d // 2) % SIDE_X, d % 2

    def index(y, x, c):
        return ((y % SIDE_Y) * SIDE_X + x % SIDE_X) * 2 + c

    def go(block, dy, dx, flip=0):
        route = [(d, index(place(d)[0] + dy, place(d)[1] + dx, place(d)[2] ^ flip)) for d in range(parts)]
        return lax.ppermute(block, "dp", route)

    def gradient(tab, left, right, sums):
        wide = hidden + (PAD if sums else 0)
        send, keep = vmem_call(
            weight_kernel,
            [((half, wide), BF)] * 2,
            (jnp.asarray(tab), left, right, *sums),
            scratch=[pltpu.VMEM((width, rows), BF)],
            flops=2 * rows * width * hidden,
            moved=2 * width * hidden,
        )
        return keep, go(send, 0, 0, 1)

    def ring(pair, first, second):
        keep, got = pair
        wide = keep.shape[1]
        line = half // 4
        far = vmem_call(far_kernel, [((line, wide // 2), BF)] * 2, (keep, got))
        (rest,) = vmem_call(rest_kernel, [((3 * line, wide), BF)], (keep, got))
        below, above = go(far[0], *first), go(far[1], -first[0], -first[1])
        up, down = vmem_call(relay_kernel, [((line, wide), BF)] * 2, (rest, below, above))
        below, above = go(up, *first), go(down, -first[0], -first[1])
        each = line // 4
        own, *others = vmem_call(
            turn_kernel,
            [((each, wide), F32)] + [((each, wide), BF)] * 3,
            (rest, below, above),
        )
        found = [go(others[k - 1], k * second[0], k * second[1]) for k in (2, 1, 3)]
        shapes = [jax.ShapeDtypeStruct((each, hidden), F32)]
        if wide > hidden:
            shapes.append(jax.ShapeDtypeStruct((1, each), F32))
        return pl.pallas_call(
            final_kernel,
            out_shape=tuple(shapes),
            in_specs=[VMEM_SPEC] * 4,
            out_specs=(VMEM_SPEC,) * len(shapes),
            compiler_params=pltpu.CompilerParams(vmem_limit_bytes=16 * MIB),
        )(own, *found)

    pair_y = gradient(table[1], gat, act, ())
    pair_x = gradient(table[0], nrm, ghd, (gsum,))
    (out_out,) = ring(pair_y, (1, 0), (0, 1))
    out_in, out_gain = ring(pair_x, (0, 1), (1, 0))
    return out_in[None], out_out[None], out_gain


def solution(mesh):
    placed = (
        P("dp", None, None, None),
        P("dp", None, None, None),
        P("section", None, None),
        P("section", None, None),
        P("section", None),
        P("dp", None, None, None),
    )
    return jax.shard_map(
        per_device,
        mesh=mesh,
        in_specs=placed,
        out_specs=(P("section", "dp", None), P("section", "dp", None), P("section", "dp")),
        check_vma=False,
    )
```
